1024 devices in a mesh: dp: 32 (over y_hi, z), ctx: 32 (over y_lo, x, core).
Axes of the slice: x: 8, y: 8 (y_hi: 4, y_lo: 2; y = y_hi * 2 + y_lo), z: 8, core: 2. Of those that a mesh axis runs over, the one named last changes fastest.
Arguments:
- emb: bfloat16 [32, 4096, 7168], P('dp', 'ctx'), may hold values from -6 to 6
- doc_lengths: int32 [32, 64], P('dp'), may hold values from 1 to 128, 4096 in all within a row
- latent: bfloat16 [32, 4096, 512], P('dp', 'ctx'), may hold values from -4 to 4
- q_latent: bfloat16 [32, 4096, 4, 512], P('dp', 'ctx'), may hold values from -32 to 32
- q_rope: bfloat16 [32, 4096, 256], P('dp', 'ctx'), may hold values from -12 to 12
- cotangent: bfloat16 [32, 4096, 4, 512], P('dp', 'ctx'), may hold values from -6 to 6
- gain: float32 [7168], replicated, may hold values from 0.1 to 1.9
- w_rope: bfloat16 [7168, 64], replicated, may hold values from -0.0625 to 0.0625
Outputs:
- grad_latent: bfloat16 [32, 4096, 512], P('dp', 'ctx')
- grad_rope_w: float32 [7168, 64], P(('dp', 'ctx'))
The draws below stay inside these ranges and needn't reach their ends.
Inputs may be any that keep to these rules, and one draw needn't show every extreme that they name: `doc_lengths`: each sequence's lengths sum to 4096; some document has exactly 128 tokens.
All inputs are finite; a program needn't handle non-finite values.
Results may differ from the reference program's by a relative error of at most 0.014.
Values may be sent and summed in bfloat16 or wider, within the bound.
A program may use at most 32 MiB of HBM per device.

```python
import math
import jax
import jax.numpy as jnp
import numpy as np
from jax import lax

D = 7168
KVR = 512
ROPE = 64
HEADS = 4
TOK = 128
SEQS = 32
LENGTH = 4096
NDOC = 64
N_CTX = 32


def draw_pair(key):
    base = jax.random.fold_in(key, 7103)
    lat_key, query_key = jax.random.split(base, 2)
    latent = jnp.clip(jax.random.normal(lat_key, (SEQS, LENGTH, KVR), jnp.float32), -4.0, 4.0)
    queries = jnp.clip(0.5 * jax.random.normal(query_key, (SEQS, LENGTH, HEADS, KVR), jnp.float32), -3.0, 3.0)
    return (latent, queries)


def draw_latent(key, part):
    return draw_pair(key)[0].astype(jnp.bfloat16)


def draw_q_latent(key, part):
    return draw_pair(key)[1].astype(jnp.bfloat16)


def levels(own_key, shape, pieces, least, top_value):
    def one(dim, blocks):
        heights = jax.random.uniform(jax.random.fold_in(jax.random.fold_in(own_key, 6), dim), (blocks,), jnp.float32, least / len(pieces), top_value / len(pieces))
        return jnp.repeat(jnp.exp(heights), shape[dim] // blocks).reshape((-1,) + (1,) * (len(shape) - dim - 1))

    loudness = one(*pieces[0])
    for cut in pieces[1:]:
        loudness = loudness * one(*cut)
    return loudness


def split_up(amount, total, limit, slope):
    loads = [(1 << 20) // math.isqrt(rank ** slope) + 1 for rank in range(2, amount + 1)]
    spare, counts = total - limit - (amount - 1), [1] * (amount - 1)
    while spare > 0:
        free = [i for i in range(amount - 1) if counts[i] < limit]
        whole, budget = sum([loads[i] for i in free]), spare
        for i in free:
            addition = min(limit - counts[i], max(1, budget * loads[i] // whole), spare)
            counts[i] = counts[i] + addition
            spare = spare - addition
    return np.array([limit] + counts)


def ragged(stream_key, amount, total, bound, lean):
    if amount == 2:
        one = jax.random.randint(stream_key, (), max(1, total - bound), min(bound, total - 1) + 1)
        return jnp.stack([one, total - one])
    lengths = jnp.asarray(split_up(amount, total, bound, lean), jnp.int32)
    pairs = (amount - 1) // 2
    giver, sink = lengths[1:1 + 2 * pairs:2], lengths[2:2 + 2 * pairs:2]
    margin = jnp.minimum(giver - 1, bound - sink)
    moved = jax.random.randint(jax.random.fold_in(stream_key, 1), (pairs,), 0, 1 << 20) % (margin + 1)
    lengths = lengths.at[1:1 + 2 * pairs:2].set(giver - moved).at[2:2 + 2 * pairs:2].set(sink + moved)
    return lengths[jax.random.permutation(jax.random.fold_in(stream_key, 2), amount)]


def scatter_about(key, dims, scale, bound, shards=(), kind=jnp.bfloat16):
    factor_of = levels(key, dims, shards, -0.22, 0.18) if shards else 1.0
    array = jax.random.normal(key, dims, jnp.float32) * scale * factor_of
    return jnp.minimum(jnp.maximum(array, -bound), bound).astype(kind)


def setup_inputs(seed: int = 0) -> dict:
    keys = jax.random.split(jax.random.key(seed), 9)
    emb = scatter_about(keys[0], (SEQS, LENGTH, D), 1.0, 6.0, ((0, 32), (1, 32)))
    doc_lengths = jax.vmap(lambda own: ragged(own, NDOC, LENGTH, TOK, 2))(jax.random.split(keys[1], SEQS)).reshape((SEQS, NDOC)).astype(jnp.int32)
    latent = draw_latent(jax.random.fold_in(keys[8], 71), 0)
    q_latent = draw_q_latent(jax.random.fold_in(keys[8], 71), 0)
    q_rope = scatter_about(keys[4], (SEQS, LENGTH, HEADS * ROPE), 2.0, 12.0, ((0, 32), (1, 32)))
    cotangent = scatter_about(keys[5], (SEQS, LENGTH, HEADS, KVR), 1.0, 6.0, ((0, 32), (1, 32)))
    gain = jnp.clip(1.0 + 0.18 * jax.random.normal(keys[6], (D,), jnp.float32), 0.1, 1.9)
    w_rope = scatter_about(keys[7], (D, ROPE), D ** -0.5, 0.0625)
    return {"emb": emb, "doc_lengths": doc_lengths, "latent": latent, "q_latent": q_latent, "q_rope": q_rope, "cotangent": cotangent, "gain": gain, "w_rope": w_rope}


score_scale = 192.0 ** (-0.5)
norm_eps = 1e-06

def doc_lookup(doc_ends_src, places):
    doc_ends = jnp.cumsum(doc_ends_src).astype(jnp.int32)
    passed = doc_ends[None, :] <= places[:, None]
    doc_index = lax.optimization_barrier(jnp.sum(passed.astype(jnp.int32), axis=1)).astype(jnp.int32)
    doc_start = lax.optimization_barrier(jnp.sum(jnp.where(passed, doc_ends_src[None, :], 0), axis=1)).astype(jnp.int32)
    return (doc_index, doc_start)

def normed_rows(rows, keep_mask, gain):
    values = jnp.where(keep_mask[:, None], rows.astype(jnp.float32), 0.0)
    mean_sq = lax.optimization_barrier(jnp.mean(values * values, axis=1, keepdims=True))
    return (values * lax.rsqrt(mean_sq + norm_eps) * gain[None, :]).astype(jnp.bfloat16)

def rotation(positions, half_width):
    frequency = 10000.0 ** (-jnp.arange(half_width).astype(jnp.float32) / half_width)
    angles = positions.astype(jnp.float32)[:, None] * frequency[None, :]
    return (jnp.cos(angles), jnp.sin(angles))

def rotate(raw_key, cosine, sine_table, half_width):
    leading, trailing = (raw_key[:, :half_width], raw_key[:, half_width:])
    return jnp.concatenate([leading * cosine - trailing * sine_table, leading * sine_table + trailing * cosine], 1)

def unrotate(key_grad, cosine, sine_table, half_width):
    leading, trailing = (key_grad[:, :half_width], key_grad[:, half_width:])
    return jnp.concatenate([leading * cosine + trailing * sine_table, trailing * cosine - leading * sine_table], 1)

def contract_rows(left, right):
    return lax.dot_general(left, right, (((0,), (0,)), ((), ())), preferred_element_type=jnp.float32)

def contract_cols(left, right):
    return lax.dot_general(left, right, (((1,), (1,)), ((), ())), preferred_element_type=jnp.float32)

def weight_product(normed, raw_grad):
    return lax.dot_general(normed.astype(jnp.float32), raw_grad, (((0,), (0,)), ((), ())), precision=lax.Precision.HIGHEST, preferred_element_type=jnp.float32)

def key_gradients(query_lat, query_rope, cot_rows, keys_lat, keys_rope, allowed):
    scores = (contract_cols(query_lat, keys_lat) + contract_cols(query_rope, keys_rope)) * score_scale
    scores = jnp.where(allowed, scores, -1e+30)
    highest = lax.optimization_barrier(jnp.max(scores, axis=1, keepdims=True))
    exponent = jnp.where(allowed, jnp.exp(scores - highest), 0.0)
    probs = exponent / lax.optimization_barrier(jnp.sum(exponent, axis=1, keepdims=True))
    weights = probs.astype(jnp.bfloat16)
    dprobs = contract_cols(cot_rows, keys_lat)
    centre = lax.optimization_barrier(jnp.sum(probs * dprobs, axis=1, keepdims=True))
    score_grad = (score_scale * probs * (dprobs - centre)).astype(jnp.bfloat16)
    lat_grad = contract_rows(weights, cot_rows) + contract_rows(score_grad, query_lat)
    rope_grad = contract_rows(score_grad, query_rope)
    return (lat_grad, rope_grad)

def sequence_grads(items):
    emb_seq, lengths_row, lat_seq, qlat_seq, qrope_seq, cot_seq, gain, w_rope = items
    half_width = ROPE // 2
    places = jnp.arange(LENGTH).astype(jnp.int32)
    doc_index, doc_start = doc_lookup(lengths_row, places)
    next_index, unused = doc_lookup(lengths_row, places + 1)
    shifted = jnp.concatenate([emb_seq[1:], jnp.zeros_like(emb_seq[:1])], 0)
    keep_mask = (next_index == doc_index) & (places + 1 < LENGTH)
    normed = normed_rows(shifted, keep_mask, gain)
    raw_key = jnp.dot(normed, w_rope, preferred_element_type=jnp.float32)
    cosine, sine_table = rotation(places - doc_start, half_width)
    key_rope = rotate(raw_key, cosine, sine_table, half_width).astype(jnp.bfloat16)
    lat_pad = jnp.concatenate([jnp.zeros((TOK, KVR), lat_seq.dtype), lat_seq], 0)
    rope_pad = jnp.concatenate([jnp.zeros((TOK, ROPE), key_rope.dtype), key_rope], 0)

    def one_block(block):
        offset = (block * TOK).astype(jnp.int32)
        q_places = offset + jnp.arange(TOK).astype(jnp.int32)
        k_places = offset - TOK + jnp.arange(2 * TOK).astype(jnp.int32)
        q_doc, unused_q = doc_lookup(lengths_row, q_places)
        k_doc, unused_k = doc_lookup(lengths_row, k_places)
        allowed = (k_places[None, :] >= 0) & (k_places[None, :] <= q_places[:, None]) & (k_doc[None, :] == q_doc[:, None])
        allowed = jnp.repeat(allowed, HEADS, axis=0)
        query_lat = lax.dynamic_slice_in_dim(qlat_seq, offset, TOK, 0).reshape(TOK * HEADS, KVR)
        query_rope = lax.dynamic_slice_in_dim(qrope_seq, offset, TOK, 0).reshape(TOK * HEADS, ROPE)
        cot_rows = lax.dynamic_slice_in_dim(cot_seq, offset, TOK, 0).reshape(TOK * HEADS, KVR)
        keys_lat = lax.dynamic_slice_in_dim(lat_pad, offset, 2 * TOK, 0)
        keys_rope = lax.dynamic_slice_in_dim(rope_pad, offset, 2 * TOK, 0)
        return key_gradients(query_lat, query_rope, cot_rows, keys_lat, keys_rope, allowed)
    lat_parts, rope_parts = lax.map(one_block, jnp.arange(N_CTX).astype(jnp.int32))
    lat_total = lat_parts[:, TOK:] + jnp.concatenate([lat_parts[1:, :TOK], jnp.zeros_like(lat_parts[:1, :TOK])], 0)
    rope_total = rope_parts[:, TOK:] + jnp.concatenate([rope_parts[1:, :TOK], jnp.zeros_like(rope_parts[:1, :TOK])], 0)
    key_grad_raw = unrotate(rope_total.reshape(LENGTH, ROPE), cosine, sine_table, half_width)
    weight_part = weight_product(normed, key_grad_raw)
    return (lat_total.reshape(LENGTH, KVR).astype(jnp.bfloat16), weight_part)

def reference(emb, doc_lengths, latent, q_latent, q_rope, cotangent, gain, w_rope):

    def per_sequence(items):
        return sequence_grads(items + (gain, w_rope))
    grad_latent, weight_parts = lax.map(per_sequence, (emb, doc_lengths, latent, q_latent, q_rope, cotangent))
    grad_rope_w = lax.optimization_barrier(jnp.sum(weight_parts, axis=0)) * (SEQS * LENGTH) ** (-0.5)
    return (grad_latent, grad_rope_w)
```

```python
import jax
import jax.numpy as jnp
from jax import lax
from jax.experimental import pallas as pl
from jax.experimental.pallas import tpu as pltpu
from jax.sharding import PartitionSpec as P

MESH = pl.DeviceIdType.MESH
F32 = jnp.float32
BF16 = jnp.bfloat16
UNITS = (3, 2, 2)
FIRST_UNIT = (0, 3, 5)
ROW_START = (0, 768, 1280)
ORDER = (4, 3, 5, 2, 6, 1, 7)


def place():
    d, c = lax.axis_index("dp"), lax.axis_index("ctx")
    return {
        "core": c % 2,
        "x": (c // 2) % 8,
        "y": (d // 8) * 2 + c // 16,
        "z": d % 8,
    }


def device(at, **moved):
    p = {**at, **moved}
    return ((p["y"] // 2) * 8 + p["z"], ((p["y"] % 2) * 8 + p["x"]) * 2 + p["core"])


STAGES = (("x", "z", "y"), ("y", "x", "z"), ("z", "x", "y"))


def step_of(axis, i):
    if axis == "x":
        return i * 14
    if axis == "z":
        return i * 224
    return (i // 2) * 1792 + (i % 2) * 112


def transpose_rows(e_ref, et_ref):
    def body(i, carry):
        for k in range(8):
            at = pl.multiple_of(i * 1024 + k * 128, 128)
            et_ref[pl.ds(at, 128), :] = e_ref[:, pl.ds(at, 128)].astype(F32).T
        return carry

    lax.fori_loop(0, 7, body, 0)


def build_left(et_ref, left_ref):
    def body(a, carry):
        for color, (first, second, third) in enumerate(STAGES):
            units = UNITS[color]
            stride = step_of(second, 1)
            for unit in range(units):
                for q in range(2):
                    for half in range(2):
                        for pair in range(2):
                            rows = []
                            for p in (2 * pair, 2 * pair + 1):
                                base = (
                                    step_of(first, a)
                                    + step_of(third, 2 * p + half)
                                    + q * 7
                                    + FIRST_UNIT[color]
                                    + unit
                                )
                                rows.append(et_ref[pl.ds(base, 8, stride=stride), :])
                            at = ROW_START[color] + a * (units * 32) + unit * 32 + pair * 16
                            left_ref[
                                q, pl.ds(pl.multiple_of(at, 16), 16), half * 128 : half * 128 + 128
                            ] = jnp.concatenate(rows, 0).astype(BF16)
        return carry

    lax.fori_loop(0, 8, body, 0)


def rs_scratch():
    shapes = [
        pltpu.VMEM((7168, 128), F32),
        pltpu.VMEM((2, 1792, 256), BF16),
        pltpu.VMEM((1792, 128), BF16),
        pltpu.VMEM((1792, 128), BF16),
        pltpu.VMEM((1792, 128), F32),
        pltpu.SemaphoreType.DMA((3,)),
        pltpu.SemaphoreType.DMA((3,)),
        pltpu.SemaphoreType.DMA((3, 3, 8)),
        pltpu.SemaphoreType.DMA((3, 3, 8)),
    ]
    for n in UNITS:
        shapes += [
            pltpu.VMEM((8, n * 32, 128), BF16),
            pltpu.VMEM((8, n * 32, 128), BF16),
            pltpu.VMEM((n * 32, 128), F32),
            pltpu.VMEM((8, n * 4, 128), F32),
            pltpu.VMEM((8, n * 4, 128), F32),
            pltpu.VMEM((n * 4, 128), F32),
            pltpu.VMEM((4, n, 128), F32),
            pltpu.VMEM((8, n, 128), F32),
        ]
    return shapes


def greet(at, barrier):
    for axis in ("x", "y", "z"):
        for step in range(1, 8):
            pl.semaphore_signal(
                barrier,
                inc=1,
                device_id=device(at, **{axis: (at[axis] + step) % 8}),
                device_id_type=MESH,
            )
    pl.semaphore_signal(barrier, inc=1, device_id=device(at, core=1 - at["core"]), device_id_type=MESH)


GREETED = 22


def reduce_scatter(at, right, out_ref, scale, left_ref, c_send, c_recv, own, c_ss, c_rs, ss, rs, bufs):
    core = at["core"]
    partner = device(at, core=1 - core)
    pending = []
    core_copies = []
    for color, n in enumerate(UNITS):
        rows = pl.ds(ROW_START[color], n * 256)
        c_send[rows, :] = jnp.dot(
            left_ref[1 - core, rows, :], right, preferred_element_type=F32
        ).astype(BF16)
        copy = pltpu.make_async_remote_copy(
            src_ref=c_send.at[rows],
            dst_ref=c_recv.at[rows],
            send_sem=c_ss.at[color],
            recv_sem=c_rs.at[color],
            device_id=partner,
            device_id_type=MESH,
        )
        copy.start()
        core_copies.append(copy)
    own[...] = jnp.dot(left_ref[core], right, preferred_element_type=F32)

    def send(color, stage, source_of, target):
        axis = STAGES[color][stage]
        for step in ORDER:
            to = (at[axis] + step) % 8
            copy = pltpu.make_async_remote_copy(
                src_ref=source_of(to),
                dst_ref=target.at[step],
                send_sem=ss.at[color, stage, step],
                recv_sem=rs.at[color, stage, step],
                device_id=device(at, **{axis: to}),
                device_id_type=MESH,
            )
            copy.start()
            pending.append((color, stage, copy))

    def arrived(color, stage):
        for c, s, copy in pending:
            if (c, s) == (color, stage):
                copy.wait_recv()

    def total(first, target):
        value = first.astype(F32)
        for step in range(1, 8):
            value = value + target[step].astype(F32)
        return value

    for color, n in enumerate(UNITS):
        s1, r1, t1, s2, r2, t2, s3, r3 = bufs[color]
        core_copies[color].wait_recv()
        for a in range(8):
            rows = pl.ds(ROW_START[color] + a * n * 32, n * 32)
            s1[a] = (own[rows, :] + c_recv[rows, :].astype(F32)).astype(BF16)
        send(color, 0, lambda to: s1.at[to], r1)
    for color, n in enumerate(UNITS):
        s1, r1, t1, s2, r2, t2, s3, r3 = bufs[color]
        arrived(color, 0)
        t1[...] = total(s1[at[STAGES[color][0]]], r1)
        for b in range(8):
            s2[b] = t1[pl.ds(b, n * 4, stride=8), :]
        send(color, 1, lambda to: s2.at[to], r2)
    for color, n in enumerate(UNITS):
        s1, r1, t1, s2, r2, t2, s3, r3 = bufs[color]
        arrived(color, 1)
        t2[...] = total(s2[at[STAGES[color][1]]], r2)
        for p in range(4):
            s3[p] = t2[pl.ds(p, n, stride=4), :]
        send(color, 2, lambda to: s3.at[to // 2], r3)
    for color, n in enumerate(UNITS):
        s1, r1, t1, s2, r2, t2, s3, r3 = bufs[color]
        arrived(color, 2)
        last = at[STAGES[color][2]]
        value = total(s3[last // 2], r3) * scale
        value = jnp.where(last % 2 == 0, value, pltpu.roll(value, 64, 1))
        out_ref[FIRST_UNIT[color] : FIRST_UNIT[color] + n, :] = value[:, :64]
    for copy in core_copies:
        copy.wait_send()
    for _, _, copy in pending:
        copy.wait_send()


def rs_kernel(scale, e_ref, g_ref, out_ref, et, left, c_send, c_recv, own, c_ss, c_rs, ss, rs, *bufs):
    at = place()
    barrier = pltpu.get_barrier_semaphore()
    greet(at, barrier)
    transpose_rows(e_ref, et)
    build_left(et, left)
    g = g_ref[...]
    lane = lax.broadcasted_iota(jnp.int32, g.shape, 1)
    right = jnp.concatenate(
        [jnp.where(lane < 64, g, 0.0), jnp.where(lane < 64, 0.0, g)], 0
    ).astype(BF16)
    pl.semaphore_wait(barrier, GREETED)
    bufs = [bufs[8 * i : 8 * i + 8] for i in range(3)]
    reduce_scatter(at, right, out_ref, scale, left, c_send, c_recv, own, c_ss, c_rs, ss, rs, bufs)


def weight_gradient(normed, raw_grad, scale):
    return pl.pallas_call(
        lambda *refs: rs_kernel(scale, *refs),
        out_shape=jax.ShapeDtypeStruct((7, 64), F32),
        in_specs=[pl.BlockSpec(memory_space=pltpu.VMEM)] * 2,
        out_specs=pl.BlockSpec(memory_space=pltpu.VMEM),
        scratch_shapes=rs_scratch(),
        compiler_params=pltpu.CompilerParams(
            collective_id=0, has_side_effects=True, vmem_limit_bytes=60 * 1024 * 1024
        ),
        name="weight_gradient",
    )(normed, jnp.concatenate([raw_grad, raw_grad], 1))


score_scale = 192.0 ** (-0.5)
norm_eps = 1e-06


def from_behind(block, axis, distance):
    devices = range(lax.axis_size(axis))
    route = [(i - distance, i) for i in devices if i - distance in devices]
    return lax.ppermute(block, axis, route)


def doc_lookup(doc_ends_src, places):
    doc_ends = jnp.cumsum(doc_ends_src)
    passed = doc_ends[None, :] <= places[:, None]
    doc_index = jnp.sum(passed.astype(jnp.int32), axis=1)
    doc_start = jnp.sum(jnp.where(passed, doc_ends_src[None, :], 0), axis=1)
    return (doc_index, doc_start)


def normed_rows(rows, keep_mask, gain):
    values = jnp.where(keep_mask[:, None], rows.astype(jnp.float32), 0.0)
    mean_sq = jnp.mean(values * values, axis=1, keepdims=True)
    return (values * lax.rsqrt(mean_sq + norm_eps) * gain[None, :]).astype(jnp.bfloat16)


def rotation(positions, half_width):
    frequency = 10000.0 ** (-jnp.arange(half_width).astype(jnp.float32) / half_width)
    angles = positions.astype(jnp.float32)[:, None] * frequency[None, :]
    return (jnp.cos(angles), jnp.sin(angles))


def rotate(raw_key, cosine, sine_table, half_width):
    leading, trailing = (raw_key[:, :half_width], raw_key[:, half_width:])
    return jnp.concatenate(
        [leading * cosine - trailing * sine_table, leading * sine_table + trailing * cosine], 1
    )


def unrotate(key_grad, cosine, sine_table, half_width):
    leading, trailing = (key_grad[:, :half_width], key_grad[:, half_width:])
    return jnp.concatenate(
        [leading * cosine + trailing * sine_table, trailing * cosine - leading * sine_table], 1
    )


def contract_rows(left, right):
    return lax.dot_general(
        left, right, (((0,), (0,)), ((), ())), preferred_element_type=jnp.float32
    )


def contract_cols(left, right):
    return lax.dot_general(
        left, right, (((1,), (1,)), ((), ())), preferred_element_type=jnp.float32
    )


def key_gradients(query_lat, query_rope, cot_rows, keys_lat, keys_rope, allowed):
    scores = (
        contract_cols(query_lat, keys_lat) + contract_cols(query_rope, keys_rope)
    ) * score_scale
    scores = jnp.where(allowed, scores, -1e30)
    highest = jnp.max(scores, axis=1, keepdims=True)
    exponent = jnp.where(allowed, jnp.exp(scores - highest), 0.0)
    probs = exponent / jnp.sum(exponent, axis=1, keepdims=True)
    weights = probs.astype(jnp.bfloat16)
    dprobs = contract_cols(cot_rows, keys_lat)
    centre = jnp.sum(probs * dprobs, axis=1, keepdims=True)
    score_grad = (score_scale * probs * (dprobs - centre)).astype(jnp.bfloat16)
    lat_grad = contract_rows(weights, cot_rows) + contract_rows(score_grad, query_lat)
    rope_grad = contract_rows(score_grad, query_rope)
    return (lat_grad, rope_grad)


def per_device(emb, doc_lengths, latent, q_latent, q_rope, cotangent, gain, w_rope):
    tokens_here = emb.shape[1]
    head_count = q_latent.shape[2]
    lat_width = latent.shape[2]
    rope_width = w_rope.shape[1]
    half_width = rope_width // 2
    ctx_count = lax.axis_size("ctx")
    data_count = lax.axis_size("dp")
    seq_length = tokens_here * ctx_count
    offset = lax.axis_index("ctx") * tokens_here
    lengths_row = doc_lengths[0]
    places = offset + jnp.arange(tokens_here, dtype=jnp.int32)
    doc_index, doc_start = doc_lookup(lengths_row, places)
    next_index, unused_start = doc_lookup(lengths_row, places + 1)
    incoming = from_behind(emb[0, :1, :], "ctx", -1)
    shifted = jnp.concatenate([emb[0, 1:, :], incoming], 0)
    keep_mask = (next_index == doc_index) & (places + 1 < seq_length)
    normed = normed_rows(shifted, keep_mask, gain)
    raw_key = jnp.dot(normed, w_rope, preferred_element_type=jnp.float32)
    cosine, sine_table = rotation(places - doc_start, half_width)
    key_rope = rotate(raw_key, cosine, sine_table, half_width).astype(jnp.bfloat16)
    own_lat = latent[0]
    prev_lat, prev_rope = from_behind((own_lat, key_rope), "ctx", 1)
    k_places = offset - tokens_here + jnp.arange(2 * tokens_here, dtype=jnp.int32)
    k_doc, unused_kstart = doc_lookup(lengths_row, k_places)
    allowed = (
        (k_places[None, :] >= 0)
        & (k_places[None, :] <= places[:, None])
        & (k_doc[None, :] == doc_index[:, None])
    )
    allowed = jnp.repeat(allowed, head_count, axis=0)
    query_lat = q_latent[0].reshape(tokens_here * head_count, lat_width)
    query_rope = q_rope[0].reshape(tokens_here * head_count, rope_width)
    cot_rows = cotangent[0].reshape(tokens_here * head_count, lat_width)
    keys_lat = jnp.concatenate([prev_lat, own_lat], 0)
    keys_rope = jnp.concatenate([prev_rope, key_rope], 0)
    lat_grad, rope_grad = key_gradients(
        query_lat, query_rope, cot_rows, keys_lat, keys_rope, allowed
    )
    back_lat, back_rope = from_behind((lat_grad[:tokens_here], rope_grad[:tokens_here]), "ctx", -1)
    lat_total = lat_grad[tokens_here:] + back_lat
    rope_total = rope_grad[tokens_here:] + back_rope
    grad_latent = lat_total.astype(jnp.bfloat16)[None]
    key_grad_raw = unrotate(rope_total, cosine, sine_table, half_width)
    loss_scale = float(data_count * seq_length) ** (-0.5)
    grad_rope_w = weight_gradient(normed, key_grad_raw, loss_scale)
    return (grad_latent, grad_rope_w)


def solution(mesh):
    placed = (
        P("dp", "ctx", None),
        P("dp", None),
        P("dp", "ctx", None),
        P("dp", "ctx", None, None),
        P("dp", "ctx", None),
        P("dp", "ctx", None, None),
        P(),
        P(),
    )
    return jax.shard_map(
        per_device,
        mesh=mesh,
        in_specs=placed,
        out_specs=(P("dp", "ctx", None), P(("dp", "ctx"), None)),
        check_vma=False,
    )
```

```python
import numpy as np
import jax
import jax.numpy as jnp
from jax import lax
from jax.experimental import pallas as pl
from jax.experimental.pallas import tpu as pltpu
from jax.sharding import PartitionSpec as P

MESH = pl.DeviceIdType.MESH
F32 = jnp.float32
BF16 = jnp.bfloat16
UNITS = (1, 3, 3)
FIRST_UNIT = (0, 1, 4)
ROW_START = (0, 256, 1024)
SENDING = (1, 2, 0)
ORDER = (4, 3, 5, 2, 6, 1, 7)


def place():
    d, c = lax.axis_index("dp"), lax.axis_index("ctx")
    return {
        "core": c % 2,
        "x": (c // 2) % 8,
        "y": (d // 8) * 2 + c // 16,
        "z": d % 8,
    }


def device(at, **moved):
    p = {**at, **moved}
    return ((p["y"] // 2) * 8 + p["z"], ((p["y"] % 2) * 8 + p["x"]) * 2 + p["core"])


STAGES = (("x", "z", "y"), ("y", "x", "z"), ("z", "x", "y"))


def step_of(axis, i):
    if axis == "x":
        return i * 14
    if axis == "z":
        return i * 224
    return (i // 2) * 1792 + (i % 2) * 112


def build_left(et_ref, left_ref):
    def body(a, carry):
        for color, (first, second, third) in enumerate(STAGES):
            units = UNITS[color]
            stride = step_of(second, 1)
            for unit in range(units):
                for q in range(2):
                    for half in range(2):
                        for pair in range(2):
                            rows = []
                            for p in (2 * pair, 2 * pair + 1):
                                base = (
                                    step_of(first, a)
                                    + step_of(third, 2 * p + half)
                                    + q * 7
                                    + FIRST_UNIT[color]
                                    + unit
                                )
                                rows.append(et_ref[pl.ds(base, 8, stride=stride), :])
                            at = ROW_START[color] + a * (units * 32) + unit * 32 + pair * 16
                            left_ref[
                                q, pl.ds(pl.multiple_of(at, 16), 16), half * 128 : half * 128 + 128
                            ] = jnp.concatenate(rows, 0).astype(BF16)
        return carry

    lax.fori_loop(0, 8, body, 0)


def rs_scratch():
    shapes = [
        pltpu.VMEM((7168, 128), F32),
        pltpu.VMEM((2, 1792, 256), BF16),
        pltpu.VMEM((1792, 128), BF16),
        pltpu.VMEM((1792, 128), BF16),
        pltpu.VMEM((1792, 128), F32),
        pltpu.SemaphoreType.DMA((3,)),
        pltpu.SemaphoreType.DMA((3,)),
        pltpu.SemaphoreType.DMA((3, 3, 8)),
        pltpu.SemaphoreType.DMA((3, 3, 8)),
    ]
    for n in UNITS:
        shapes += [
            pltpu.VMEM((8, n * 32, 128), BF16),
            pltpu.VMEM((8, n * 32, 128), BF16),
            pltpu.VMEM((n * 32, 128), F32),
            pltpu.VMEM((8, n * 4, 128), BF16),
            pltpu.VMEM((8, n * 4, 128), BF16),
            pltpu.VMEM((n * 4, 128), F32),
            pltpu.VMEM((4, n, 128), F32),
            pltpu.VMEM((8, n, 128), F32),
        ]
    return shapes


def greet(at, barrier):
    for axis in ("x", "y", "z"):
        for step in range(1, 8):
            pl.semaphore_signal(
                barrier,
                inc=1,
                device_id=device(at, **{axis: (at[axis] + step) % 8}),
                device_id_type=MESH,
            )
    pl.semaphore_signal(barrier, inc=1, device_id=device(at, core=1 - at["core"]), device_id_type=MESH)


GREETED = 22


def reduce_scatter(
    at, right, out_ref, scale, left_ref, c_send, c_recv, own, c_ss, c_rs, ss, rs, bufs, under_first, under_second
):
    core = at["core"]
    partner = device(at, core=1 - core)
    pending = []
    core_copies = {}
    for color in SENDING:
        n = UNITS[color]
        rows = pl.ds(ROW_START[color], n * 256)
        c_send[rows, :] = jnp.dot(
            left_ref[1 - core, rows, :], right, preferred_element_type=F32
        ).astype(BF16)
        copy = pltpu.make_async_remote_copy(
            src_ref=c_send.at[rows],
            dst_ref=c_recv.at[rows],
            send_sem=c_ss.at[color],
            recv_sem=c_rs.at[color],
            device_id=partner,
            device_id_type=MESH,
        )
        copy.start()
        core_copies[color] = copy
    own[...] = jnp.dot(left_ref[core], right, preferred_element_type=F32)

    def send(color, stage, source_of, target):
        axis = STAGES[color][stage]
        for step in ORDER:
            to = (at[axis] + step) % 8
            copy = pltpu.make_async_remote_copy(
                src_ref=source_of(to),
                dst_ref=target.at[step],
                send_sem=ss.at[color, stage, step],
                recv_sem=rs.at[color, stage, step],
                device_id=device(at, **{axis: to}),
                device_id_type=MESH,
            )
            copy.start()
            pending.append((color, stage, copy))

    def arrived(color, stage):
        for c, s, copy in pending:
            if (c, s) == (color, stage):
                copy.wait_recv()

    def total(first, target):
        value = first.astype(F32)
        for step in range(1, 8):
            value = value + target[step].astype(F32)
        return value

    for color in SENDING:
        n = UNITS[color]
        s1, r1, t1, s2, r2, t2, s3, r3 = bufs[color]
        core_copies[color].wait_recv()
        for a in range(8):
            rows = pl.ds(ROW_START[color] + a * n * 32, n * 32)
            s1[a] = (own[rows, :] + c_recv[rows, :].astype(F32)).astype(BF16)
        send(color, 0, lambda to: s1.at[to], r1)
    under_first()
    for color, n in enumerate(UNITS):
        s1, r1, t1, s2, r2, t2, s3, r3 = bufs[color]
        arrived(color, 0)
        t1[...] = total(s1[at[STAGES[color][0]]], r1)
        for b in range(8):
            s2[b] = t1[pl.ds(b, n * 4, stride=8), :].astype(BF16)
        send(color, 1, lambda to: s2.at[to], r2)
    under_second()
    for color, n in enumerate(UNITS):
        s1, r1, t1, s2, r2, t2, s3, r3 = bufs[color]
        arrived(color, 1)
        t2[...] = total(s2[at[STAGES[color][1]]], r2)
        for p in range(4):
            s3[p] = t2[pl.ds(p, n, stride=4), :]
        send(color, 2, lambda to: s3.at[to // 2], r3)
    for color, n in enumerate(UNITS):
        s1, r1, t1, s2, r2, t2, s3, r3 = bufs[color]
        arrived(color, 2)
        last = at[STAGES[color][2]]
        value = total(s3[last // 2], r3) * scale
        value = jnp.where(last % 2 == 0, value, pltpu.roll(value, 64, 1))
        out_ref[FIRST_UNIT[color] : FIRST_UNIT[color] + n, :] = value[:, :64]
    for copy in core_copies.values():
        copy.wait_send()
    for _, _, copy in pending:
        copy.wait_send()


score_scale = 192.0 ** (-0.5)
norm_eps = 1e-06
MERGED = 3


def rotary_tables():
    frequency = (10000.0 ** (-np.arange(32, dtype=np.float32) / 32)).astype(np.float32)
    angles = np.arange(128, dtype=np.float32)[:, None] * frequency[None, :]
    cosine = np.cos(angles.astype(np.float64)).astype(np.float32)
    sine = np.sin(angles.astype(np.float64)).astype(np.float32)
    rest = np.concatenate([np.tile(cosine, 4), -sine, sine, -sine, sine], 1)
    parts = []
    for _ in range(3):
        part = rest.astype(jnp.bfloat16)
        parts.append(part)
        rest = rest - part.astype(np.float32)
    return np.concatenate(parts, 1)


def cols(left, right):
    return lax.dot_general(left, right, (((1,), (1,)), ((), ())), preferred_element_type=F32)


def halves(value):
    low = lax.broadcasted_iota(jnp.int32, value.shape, 1) < 64
    return jnp.where(low, value, 0.0), jnp.where(low, 0.0, value)


def pack(value):
    low = lax.broadcasted_iota(jnp.int32, (64, 128), 1) < 64
    return jnp.where(low, value[:64], value[64:128])


def unpack(value):
    low = lax.broadcasted_iota(jnp.int32, (64, 128), 1) < 64
    other = pltpu.roll(value, 64, 1)
    return jnp.concatenate([jnp.where(low, value, other), jnp.where(low, other, value)], 0)


def fused_kernel(
    scale,
    lengths_hbm,
    table_hbm,
    gain_hbm,
    emb_hbm,
    w_hbm,
    lat_hbm,
    q_hbm,
    qr_hbm,
    cot_hbm,
    outlat_ref,
    outw_ref,
    lengths_ref,
    table_ref,
    gain_ref,
    emb,
    w_t,
    keys,
    q_in,
    qr,
    cot_in,
    q_all,
    cot_all,
    kr_send,
    kr_recv,
    kr1_send,
    kr1_recv,
    kg_send,
    kg_recv,
    kg1_send,
    kg1_recv,
    lg_send,
    lg_recv,
    lg_own,
    s_all,
    d_all,
    w_all,
    sg_all,
    local_sem,
    ns,
    nr,
    et,
    left,
    c_send,
    c_recv,
    own,
    c_ss,
    c_rs,
    ss,
    rs,
    *bufs,
):
    at = place()
    dp, ctx = lax.axis_index("dp"), lax.axis_index("ctx")
    after, before = (dp, (ctx + 1) % 32), (dp, (ctx + 31) % 32)
    loads = []
    pairs = (
        (lengths_hbm, lengths_ref),
        (gain_hbm, gain_ref),
        (emb_hbm, emb),
        (w_hbm, w_t),
        (table_hbm, table_ref),
        (lat_hbm, keys.at[128:256]),
        (q_hbm, q_in),
        (cot_hbm, cot_in),
        (qr_hbm, qr),
    )
    for i, (source, target) in enumerate(pairs):
        copy = pltpu.make_async_copy(source, target, local_sem.at[i])
        copy.start()
        loads.append(copy)
    barrier = pltpu.get_barrier_semaphore()
    greet(at, barrier)
    for near in (after, before):
        pl.semaphore_signal(barrier, inc=1, device_id=near, device_id_type=MESH)

    hops = []

    def hand(source, target, to):
        i = len(hops)
        copy = pltpu.make_async_remote_copy(
            src_ref=source,
            dst_ref=target,
            send_sem=ns.at[i],
            recv_sem=nr.at[i],
            device_id=to,
            device_id_type=MESH,
        )
        copy.start()
        hops.append(copy)

    offset = ctx * 128
    loads[0].wait()
    lengths = lengths_ref[...].astype(F32)
    sub64 = lax.broadcasted_iota(jnp.int32, (64, 64), 0)
    lane64 = lax.broadcasted_iota(jnp.int32, (64, 64), 1)
    ends = jnp.sum(jnp.where(lane64 <= sub64, lengths, 0.0), 1, keepdims=True)
    place_row = (offset + lax.broadcasted_iota(jnp.int32, (1, 128), 1)).astype(F32)
    start_row = jnp.max(jnp.where(ends <= place_row, ends, 0.0), 0, keepdims=True)
    shift_start = jnp.max(jnp.where(ends <= place_row - 1.0, ends, 0.0), 0, keepdims=True)
    ended = jnp.max(jnp.where(ends == place_row, 1.0, 0.0), 0, keepdims=True)
    keep_row = jnp.where((place_row >= 1.0) & (place_row < 4096.0), 1.0 - ended, 0.0)
    sub = lax.broadcasted_iota(jnp.int32, (128, 128), 0)
    lane = lax.broadcasted_iota(jnp.int32, (128, 128), 1)
    eye = sub == lane
    start_col = jnp.sum(jnp.where(eye, shift_start, 0.0), 1, keepdims=True)
    keep = jnp.sum(jnp.where(eye, keep_row, 0.0), 1, keepdims=True) > 0.5
    pos_lane = (offset - 1 + sub).astype(F32) - start_col
    chosen = jnp.where(pos_lane == lane.astype(F32), 1.0, 0.0).astype(BF16)

    loads[1].wait()
    loads[2].wait()
    loads[3].wait()

    def spans(i):
        for k in range(8):
            yield pl.ds(pl.multiple_of(i * 1024 + k * 128, 128), 128)

    def prepare(turned):
        def body(i, squares):
            for span in spans(i):
                scale_here = gain_ref[:, span]
                w_t[:, span] = (w_t[:, span].astype(F32) * scale_here).astype(BF16)
                value = emb[:, span].astype(F32)
                squares = squares + value * value
                if turned:
                    et[span, :] = (value * scale_here).T
            return squares

        return body

    def turn(i, carry):
        for span in spans(i):
            et[span, :] = (emb[:, span].astype(F32) * gain_ref[:, span]).T
        return carry

    squares = lax.fori_loop(0, MERGED, prepare(True), jnp.zeros((128, 128), F32))
    squares = lax.fori_loop(MERGED, 7, prepare(False), squares)
    raw = cols(emb[...], w_t[...])
    inverse = lax.rsqrt(jnp.sum(squares, 1, keepdims=True) / 7168.0 + norm_eps)
    loads[4].wait()
    table = jnp.dot(chosen, table_ref[...], preferred_element_type=F32)
    table = table[:, :256] + table[:, 256:512] + table[:, 512:]
    cosine, sine = table[:, :128], table[:, 128:]
    raw = raw * inverse
    raw = jnp.where(keep, jnp.concatenate([raw, raw], 1), 0.0)
    key_rope = (raw * cosine + pltpu.roll(raw, 32, 1) * sine).astype(BF16).astype(F32)
    kr_send[...] = pack(key_rope).astype(BF16)
    kr1_send[...] = key_rope[0:8]
    pl.semaphore_wait(barrier, GREETED + 2)
    hand(kr_send, kr_recv, after)
    hand(kr1_send, kr1_recv, before)
    hand(lat_hbm, keys.at[0:128], after)

    for i in (5, 6, 7, 8):
        loads[i].wait()
    q_all[...] = pltpu.einshape("thd->htd", q_in[...]).reshape(512, 512)
    cot_all[...] = pltpu.einshape("thd->htd", cot_in[...]).reshape(512, 512)
    s_all[128:256, :] = cols(keys[128:256, :], q_all[...])
    d_all[128:256, :] = cols(keys[128:256, :], cot_all[...])

    hops[2].wait_recv()
    s_all[0:128, :] = cols(keys[0:128, :], q_all[...])
    d_all[0:128, :] = cols(keys[0:128, :], cot_all[...])
    hops[0].wait_recv()
    hops[1].wait_recv()
    all_rope = jnp.concatenate([unpack(kr_recv[...].astype(F32)), key_rope], 0)
    final = lax.broadcasted_iota(jnp.int32, (256, 128), 0) == 255
    all_rope = jnp.where(final, kr1_recv[0:1, :], pltpu.roll(all_rope, 255, 0))
    ropes = [h.astype(BF16) for h in halves(all_rope)]
    key_place = (offset - 128 + lax.broadcasted_iota(jnp.int32, (256, 128), 0)).astype(F32)
    allowed = (key_place >= start_row) & (key_place <= place_row)
    parts = [jnp.zeros((256, 128), F32)] * 2
    for h in range(4):
        span = slice(h * 128, h * 128 + 128)
        query_rope = qr[:, (h // 2) * 128 : (h // 2) * 128 + 128]
        score = (s_all[:, span] + cols(ropes[h % 2], query_rope)) * score_scale
        score = jnp.where(allowed, score, -1e30)
        highest = jnp.max(score, 0, keepdims=True)
        exponent = jnp.where(allowed, jnp.exp(score - highest), 0.0)
        probs = exponent / jnp.sum(exponent, 0, keepdims=True)
        w_all[:, span] = probs.astype(BF16)
        dprobs = d_all[:, span]
        centre = jnp.sum(probs * dprobs, 0, keepdims=True)
        score_grad = (score_scale * probs * (dprobs - centre)).astype(BF16)
        sg_all[:, span] = score_grad
        parts[h % 2] = parts[h % 2] + jnp.dot(score_grad, query_rope, preferred_element_type=F32)
    wide = lax.broadcasted_iota(jnp.int32, (256, 128), 1)
    key_grad = jnp.where(wide < 64, parts[0], parts[1])
    key_grad = key_grad + pltpu.roll(key_grad, 64, 1)
    kg_send[...] = pack(key_grad[:128])
    kg1_send[...] = key_grad[248:]
    hand(kg_send, kg_recv, before)
    hand(kg1_send, kg1_recv, after)
    shifted_grad = pltpu.roll(key_grad, 1, 0)[128:]

    lax.fori_loop(MERGED, 7, turn, 0)
    build_left(et, left)

    hops[3].wait_recv()
    hops[4].wait_recv()
    handed = pltpu.roll(unpack(kg_recv[...]), 1, 0)
    shifted_grad = shifted_grad + jnp.where(sub == 0, kg1_recv[7:8, :], handed)
    raw_grad = shifted_grad * cosine - pltpu.roll(shifted_grad, 32, 1) * sine
    raw_grad = jnp.where(keep, raw_grad, 0.0) * inverse
    right = jnp.concatenate(halves(raw_grad), 0).astype(BF16)

    def latent_part():
        for half in range(2):
            span = slice(half * 128, half * 128 + 128)
            part = jnp.dot(w_all[span, :], cot_all[...], preferred_element_type=F32)
            part = part + jnp.dot(sg_all[span, :], q_all[...], preferred_element_type=F32)
            if half == 0:
                lg_send[...] = part.astype(BF16)
                hand(lg_send, lg_recv, before)
            else:
                lg_own[...] = part

    def latent_out():
        hops[5].wait_recv()
        outlat_ref[...] = (lg_own[...] + lg_recv[...].astype(F32)).astype(BF16)

    bufs = [bufs[8 * i : 8 * i + 8] for i in range(3)]
    reduce_scatter(
        at, right, outw_ref, scale, left, c_send, c_recv, own, c_ss, c_rs, ss, rs, bufs, latent_part, latent_out
    )
    for hop in hops:
        hop.wait_send()


def per_device(emb, doc_lengths, latent, q_latent, q_rope, cotangent, gain, w_rope):
    loss_scale = float(32 * 4096) ** (-0.5)
    vmem = pl.BlockSpec(memory_space=pltpu.VMEM)
    hbm = pl.BlockSpec(memory_space=pl.ANY)
    grad_latent, grad_rope_w = pl.pallas_call(
        lambda *refs: fused_kernel(loss_scale, *refs),
        out_shape=(
            pltpu.VMEM((128, 512), BF16),
            pltpu.VMEM((7, 64), F32),
        ),
        in_specs=[hbm] * 9,
        out_specs=(vmem, vmem),
        scratch_shapes=[
            pltpu.VMEM((1, 64), jnp.int32),
            pltpu.VMEM((128, 768), BF16),
            pltpu.VMEM((1, 7168), F32),
            pltpu.VMEM((128, 7168), BF16),
            pltpu.VMEM((64, 7168), BF16),
            pltpu.VMEM((256, 512), BF16),
            pltpu.VMEM((128, 4, 512), BF16),
            pltpu.VMEM((128, 256), BF16),
            pltpu.VMEM((128, 4, 512), BF16),
            pltpu.VMEM((512, 512), BF16),
            pltpu.VMEM((512, 512), BF16),
            pltpu.VMEM((64, 128), BF16),
            pltpu.VMEM((64, 128), BF16),
            pltpu.VMEM((8, 128), F32),
            pltpu.VMEM((8, 128), F32),
            pltpu.VMEM((64, 128), F32),
            pltpu.VMEM((64, 128), F32),
            pltpu.VMEM((8, 128), F32),
            pltpu.VMEM((8, 128), F32),
            pltpu.VMEM((128, 512), BF16),
            pltpu.VMEM((128, 512), BF16),
            pltpu.VMEM((128, 512), F32),
            pltpu.VMEM((256, 512), F32),
            pltpu.VMEM((256, 512), F32),
            pltpu.VMEM((256, 512), BF16),
            pltpu.VMEM((256, 512), BF16),
            pltpu.SemaphoreType.DMA((9,)),
            pltpu.SemaphoreType.DMA((6,)),
            pltpu.SemaphoreType.DMA((6,)),
        ]
        + rs_scratch(),
        compiler_params=pltpu.CompilerParams(
            collective_id=0, has_side_effects=True, vmem_limit_bytes=60 * 1024 * 1024
        ),
        name="fused",
    )(
        doc_lengths,
        jnp.asarray(rotary_tables()),
        gain[None],
        emb[0],
        w_rope.T,
        latent[0],
        q_latent[0],
        q_rope[0],
        cotangent[0],
    )
    return (grad_latent[None], grad_rope_w)


def solution(mesh):
    placed = (
        P("dp", "ctx", None),
        P("dp", None),
        P("dp", "ctx", None),
        P("dp", "ctx", None, None),
        P("dp", "ctx", None),
        P("dp", "ctx", None, None),
        P(),
        P(),
    )
    return jax.shard_map(
        per_device,
        mesh=mesh,
        in_specs=placed,
        out_specs=(P("dp", "ctx", None), P(("dp", "ctx"), None)),
        check_vma=False,
    )
```

```python
import numpy as np
import jax
import jax.numpy as jnp
from jax import lax
from jax.experimental import pallas as pl
from jax.experimental.pallas import tpu as pltpu
from jax.sharding import PartitionSpec as P

MESH = pl.DeviceIdType.MESH
F32 = jnp.float32
BF16 = jnp.bfloat16
UNITS = (2, 3, 2)
FIRST_UNIT = (0, 2, 5)
ROW_START = (0, 512, 1280)
SENDING = (1, 2, 0)
ORDER = (4, 3, 5, 2, 6, 1, 7)


def place():
    d, c = lax.axis_index("dp"), lax.axis_index("ctx")
    return {
        "core": c % 2,
        "x": (c // 2) % 8,
        "y": (d // 8) * 2 + c // 16,
        "z": d % 8,
    }


def device(at, **moved):
    p = {**at, **moved}
    return ((p["y"] // 2) * 8 + p["z"], ((p["y"] % 2) * 8 + p["x"]) * 2 + p["core"])


STAGES = (
    (("x", "z", "y"), ("y", "x", "z"), ("z", "x", "y")),
    (("x", "z", "y"), ("z", "x", "y"), ("y", "x", "z")),
)


def step_of(axis, i):
    if axis == "x":
        return i * 14
    if axis == "z":
        return i * 224
    return (i // 2) * 1792 + (i % 2) * 112


def build_left(et_ref, left_ref):
    def body(a, carry):
        for color, units in enumerate(UNITS):
            for unit in range(units):
                for q in range(2):
                    first, second, third = STAGES[q][color]
                    stride = step_of(second, 1)
                    for half in range(2):
                        for pair in range(2):
                            rows = []
                            for p in (2 * pair, 2 * pair + 1):
                                base = (
                                    step_of(first, a)
                                    + step_of(third, 2 * p + half)
                                    + q * 7
                                    + FIRST_UNIT[color]
                                    + unit
                                )
                                rows.append(et_ref[pl.ds(base, 8, stride=stride), :])
                            at = ROW_START[color] + a * (units * 32) + unit * 32 + pair * 16
                            left_ref[
                                q, pl.ds(pl.multiple_of(at, 16), 16), half * 128 : half * 128 + 128
                            ] = jnp.concatenate(rows, 0).astype(BF16)
        return carry

    lax.fori_loop(0, 8, body, 0)


def rs_scratch():
    shapes = [
        pltpu.VMEM((7168, 128), F32),
        pltpu.VMEM((2, 1792, 256), BF16),
        pltpu.VMEM((1792, 128), BF16),
        pltpu.VMEM((1792, 128), BF16),
        pltpu.VMEM((1792, 128), F32),
        pltpu.SemaphoreType.DMA((3,)),
        pltpu.SemaphoreType.DMA((3,)),
        pltpu.SemaphoreType.DMA((3, 3, 8)),
        pltpu.SemaphoreType.DMA((3, 3, 8)),
    ]
    for n in UNITS:
        shapes += [
            pltpu.VMEM((8, n * 32, 128), BF16),
            pltpu.VMEM((8, n * 32, 128), BF16),
            pltpu.VMEM((n * 32, 128), F32),
            pltpu.VMEM((8, n * 4, 128), BF16),
            pltpu.VMEM((8, n * 4, 128), BF16),
            pltpu.VMEM((n * 4, 128), F32),
            pltpu.VMEM((4, n, 128), F32),
            pltpu.VMEM((8, n, 128), F32),
        ]
    return shapes


def greet(at, barrier):
    for step in ORDER:
        for axis in ("x", "y", "z"):
            pl.semaphore_signal(
                barrier,
                inc=1,
                device_id=device(at, **{axis: (at[axis] + step) % 8}),
                device_id_type=MESH,
            )
    pl.semaphore_signal(barrier, inc=1, device_id=device(at, core=1 - at["core"]), device_id_type=MESH)


GREETED = 22


def reduce_scatter(
    at, right, out_ref, scale, left_ref, c_send, c_recv, own, c_ss, c_rs, ss, rs, bufs, under_first, under_second, under_third
):
    core = at["core"]
    partner = device(at, core=1 - core)
    pending = []
    core_copies = {}
    for color in SENDING:
        n = UNITS[color]
        rows = pl.ds(ROW_START[color], n * 256)
        c_send[rows, :] = jnp.dot(
            left_ref[1 - core, rows, :], right, preferred_element_type=F32
        ).astype(BF16)
        copy = pltpu.make_async_remote_copy(
            src_ref=c_send.at[rows],
            dst_ref=c_recv.at[rows],
            send_sem=c_ss.at[color],
            recv_sem=c_rs.at[color],
            device_id=partner,
            device_id_type=MESH,
        )
        copy.start()
        core_copies[color] = copy

    def by_core(low, high):
        return low + core * (high - low)

    def spot(color, stage):
        return by_core(*(at[STAGES[q][color][stage]] for q in range(2)))

    def peer(color, stage, to):
        low, high = (device(at, **{STAGES[q][color][stage]: to}) for q in range(2))
        return tuple(by_core(a, b) for a, b in zip(low, high))

    def send(color, stage, source_of, target):
        for step in ORDER:
            to = (spot(color, stage) + step) % 8
            copy = pltpu.make_async_remote_copy(
                src_ref=source_of(to),
                dst_ref=target.at[step],
                send_sem=ss.at[color, stage, step],
                recv_sem=rs.at[color, stage, step],
                device_id=peer(color, stage, to),
                device_id_type=MESH,
            )
            copy.start()
            pending.append((color, stage, copy))

    def arrived(color, stage):
        for c, s, copy in pending:
            if (c, s) == (color, stage):
                copy.wait_recv()

    def total(first, target):
        value = first.astype(F32)
        for step in range(1, 8):
            value = value + target[step].astype(F32)
        return value

    for color in SENDING:
        n = UNITS[color]
        s1, r1, t1, s2, r2, t2, s3, r3 = bufs[color]
        span = pl.ds(ROW_START[color], n * 256)
        own[span, :] = jnp.dot(left_ref[core, span, :], right, preferred_element_type=F32)
        core_copies[color].wait_recv()
        for a in range(8):
            rows = pl.ds(ROW_START[color] + a * n * 32, n * 32)
            s1[a] = (own[rows, :] + c_recv[rows, :].astype(F32)).astype(BF16)
        send(color, 0, lambda to: s1.at[to], r1)
    under_first()
    for color, n in enumerate(UNITS):
        s1, r1, t1, s2, r2, t2, s3, r3 = bufs[color]
        arrived(color, 0)
        t1[...] = total(s1[spot(color, 0)], r1)
        for b in range(8):
            s2[b] = t1[pl.ds(b, n * 4, stride=8), :].astype(BF16)
        send(color, 1, lambda to: s2.at[to], r2)
    under_second()
    for color, n in enumerate(UNITS):
        s1, r1, t1, s2, r2, t2, s3, r3 = bufs[color]
        arrived(color, 1)
        t2[...] = total(s2[spot(color, 1)], r2)
        for p in range(4):
            s3[p] = t2[pl.ds(p, n, stride=4), :]
        send(color, 2, lambda to: s3.at[to // 2], r3)
    for copy in core_copies.values():
        copy.wait_send()
    for color, stage, copy in pending:
        if stage < 2:
            copy.wait_send()
    under_third()
    for color, n in enumerate(UNITS):
        s1, r1, t1, s2, r2, t2, s3, r3 = bufs[color]
        arrived(color, 2)
        last = spot(color, 2)
        value = total(s3[last // 2], r3) * scale
        value = jnp.where(last % 2 == 0, value, pltpu.roll(value, 64, 1))
        out_ref[FIRST_UNIT[color] : FIRST_UNIT[color] + n, :] = value[:, :64]
    for color, stage, copy in pending:
        if stage == 2:
            copy.wait_send()


score_scale = 192.0 ** (-0.5)
norm_eps = 1e-06
MERGED = 2


def rotary_tables():
    frequency = (10000.0 ** (-np.arange(32, dtype=np.float32) / 32)).astype(np.float32)
    angles = np.arange(128, dtype=np.float32)[:, None] * frequency[None, :]
    cosine = np.cos(angles.astype(np.float64)).astype(np.float32)
    sine = np.sin(angles.astype(np.float64)).astype(np.float32)
    rest = np.concatenate([np.tile(cosine, 4), -sine, sine, -sine, sine], 1)
    parts = []
    for _ in range(3):
        part = rest.astype(jnp.bfloat16)
        parts.append(part)
        rest = rest - part.astype(np.float32)
    return np.concatenate(parts, 1)


def cols(left, right):
    return lax.dot_general(left, right, (((1,), (1,)), ((), ())), preferred_element_type=F32)


def halves(value):
    low = lax.broadcasted_iota(jnp.int32, value.shape, 1) < 64
    return jnp.where(low, value, 0.0), jnp.where(low, 0.0, value)


def pack(value):
    low = lax.broadcasted_iota(jnp.int32, (64, 128), 1) < 64
    return jnp.where(low, value[:64], value[64:128])


def unpack(value):
    low = lax.broadcasted_iota(jnp.int32, (64, 128), 1) < 64
    other = pltpu.roll(value, 64, 1)
    return jnp.concatenate([jnp.where(low, value, other), jnp.where(low, other, value)], 0)


def fused_kernel(
    scale,
    lengths_hbm,
    table_hbm,
    gain_hbm,
    emb_hbm,
    w_hbm,
    lat_hbm,
    q_hbm,
    qr_hbm,
    cot_hbm,
    outlat_ref,
    outw_ref,
    lengths_ref,
    table_ref,
    gain_ref,
    emb,
    w_t,
    keys,
    q_in,
    qr,
    cot_in,
    q_all,
    cot_all,
    kr_send,
    kr_recv,
    kr1_send,
    kr1_recv,
    kg_send,
    kg_recv,
    kg1_send,
    kg1_recv,
    lg_send,
    lg_recv,
    lg_own,
    s_all,
    d_all,
    w_all,
    sg_all,
    local_sem,
    ns,
    nr,
    et,
    left,
    c_send,
    c_recv,
    own,
    c_ss,
    c_rs,
    ss,
    rs,
    *bufs,
):
    at = place()
    dp, ctx = lax.axis_index("dp"), lax.axis_index("ctx")
    after, before = (dp, (ctx + 1) % 32), (dp, (ctx + 31) % 32)
    loads = []
    pairs = (
        (lengths_hbm, lengths_ref),
        (gain_hbm, gain_ref),
        (emb_hbm, emb),
        (w_hbm, w_t),
        (table_hbm, table_ref),
        (lat_hbm, keys.at[128:256]),
        (q_hbm, q_in),
        (cot_hbm, cot_in),
        (qr_hbm, qr),
    )
    for i, (source, target) in enumerate(pairs):
        copy = pltpu.make_async_copy(source, target, local_sem.at[i])
        copy.start()
        loads.append(copy)
    barrier = pltpu.get_barrier_semaphore()
    greet(at, barrier)
    for near in (after, before):
        pl.semaphore_signal(barrier, inc=1, device_id=near, device_id_type=MESH)

    hops = []

    def hand(source, target, to):
        i = len(hops)
        copy = pltpu.make_async_remote_copy(
            src_ref=source,
            dst_ref=target,
            send_sem=ns.at[i],
            recv_sem=nr.at[i],
            device_id=to,
            device_id_type=MESH,
        )
        copy.start()
        hops.append(copy)

    offset = ctx * 128
    loads[0].wait()
    lengths = lengths_ref[...].astype(F32)
    sub64 = lax.broadcasted_iota(jnp.int32, (64, 64), 0)
    lane64 = lax.broadcasted_iota(jnp.int32, (64, 64), 1)
    ends = jnp.sum(jnp.where(lane64 <= sub64, lengths, 0.0), 1, keepdims=True)
    place_row = (offset + lax.broadcasted_iota(jnp.int32, (1, 128), 1)).astype(F32)
    start_row = jnp.max(jnp.where(ends <= place_row, ends, 0.0), 0, keepdims=True)
    shift_start = jnp.max(jnp.where(ends <= place_row - 1.0, ends, 0.0), 0, keepdims=True)
    ended = jnp.max(jnp.where(ends == place_row, 1.0, 0.0), 0, keepdims=True)
    keep_row = jnp.where((place_row >= 1.0) & (place_row < 4096.0), 1.0 - ended, 0.0)
    sub = lax.broadcasted_iota(jnp.int32, (128, 128), 0)
    lane = lax.broadcasted_iota(jnp.int32, (128, 128), 1)
    eye = sub == lane
    start_col = jnp.sum(jnp.where(eye, shift_start, 0.0), 1, keepdims=True)
    keep = jnp.sum(jnp.where(eye, keep_row, 0.0), 1, keepdims=True) > 0.5
    pos_lane = (offset - 1 + sub).astype(F32) - start_col
    chosen = jnp.where(pos_lane == lane.astype(F32), 1.0, 0.0).astype(BF16)

    loads[1].wait()
    loads[2].wait()
    loads[3].wait()

    def spans(i):
        for k in range(8):
            yield pl.ds(pl.multiple_of(i * 1024 + k * 128, 128), 128)

    def prepare(turned):
        def body(i, squares):
            for span in spans(i):
                scale_here = gain_ref[:, span]
                w_t[:, span] = (w_t[:, span].astype(F32) * scale_here).astype(BF16)
                value = emb[:, span].astype(F32)
                squares = squares + value * value
                if turned:
                    et[span, :] = (value * scale_here).T
            return squares

        return body

    def turn(i, carry):
        for span in spans(i):
            et[span, :] = (emb[:, span].astype(F32) * gain_ref[:, span]).T
        return carry

    squares = lax.fori_loop(0, MERGED, prepare(True), jnp.zeros((128, 128), F32))
    squares = lax.fori_loop(MERGED, 7, prepare(False), squares)
    pl.semaphore_wait(barrier, GREETED + 2)
    hand(lat_hbm, keys.at[0:128], after)
    raw = cols(emb[...], w_t[...])
    inverse = lax.rsqrt(jnp.sum(squares, 1, keepdims=True) / 7168.0 + norm_eps)
    loads[4].wait()
    table = jnp.dot(chosen, table_ref[...], preferred_element_type=F32)
    table = table[:, :256] + table[:, 256:512] + table[:, 512:]
    cosine, sine = table[:, :128], table[:, 128:]
    raw = raw * inverse
    raw = jnp.where(keep, jnp.concatenate([raw, raw], 1), 0.0)
    key_rope = (raw * cosine + pltpu.roll(raw, 32, 1) * sine).astype(BF16).astype(F32)
    kr_send[...] = pack(key_rope).astype(BF16)
    kr1_send[...] = key_rope[0:8]
    hand(kr_send, kr_recv, after)
    hand(kr1_send, kr1_recv, before)

    for i in (5, 6, 7, 8):
        loads[i].wait()
    q_all[...] = pltpu.einshape("thd->htd", q_in[...]).reshape(512, 512)
    cot_all[...] = pltpu.einshape("thd->htd", cot_in[...]).reshape(512, 512)
    lax.fori_loop(MERGED, 7, turn, 0)

    hops[0].wait_recv()
    s_all[...] = cols(keys[...], q_all[...])
    d_all[...] = cols(keys[...], cot_all[...])
    hops[1].wait_recv()
    hops[2].wait_recv()
    all_rope = jnp.concatenate([unpack(kr_recv[...].astype(F32)), key_rope], 0)
    final = lax.broadcasted_iota(jnp.int32, (256, 128), 0) == 255
    all_rope = jnp.where(final, kr1_recv[0:1, :], pltpu.roll(all_rope, 255, 0))
    ropes = [h.astype(BF16) for h in halves(all_rope)]
    key_place = (offset - 128 + lax.broadcasted_iota(jnp.int32, (256, 128), 0)).astype(F32)
    allowed = (key_place >= start_row) & (key_place <= place_row)
    parts = [jnp.zeros((256, 128), F32)] * 2
    for h in range(4):
        span = slice(h * 128, h * 128 + 128)
        query_rope = qr[:, (h // 2) * 128 : (h // 2) * 128 + 128]
        score = (s_all[:, span] + cols(ropes[h % 2], query_rope)) * score_scale
        score = jnp.where(allowed, score, -1e30)
        highest = jnp.max(score, 0, keepdims=True)
        exponent = jnp.where(allowed, jnp.exp(score - highest), 0.0)
        probs = exponent / jnp.sum(exponent, 0, keepdims=True)
        w_all[:, span] = probs.astype(BF16)
        dprobs = d_all[:, span]
        centre = jnp.sum(probs * dprobs, 0, keepdims=True)
        score_grad = (score_scale * probs * (dprobs - centre)).astype(BF16)
        sg_all[:, span] = score_grad
        parts[h % 2] = parts[h % 2] + jnp.dot(score_grad, query_rope, preferred_element_type=F32)
    wide = lax.broadcasted_iota(jnp.int32, (256, 128), 1)
    key_grad = jnp.where(wide < 64, parts[0], parts[1])
    key_grad = key_grad + pltpu.roll(key_grad, 64, 1)
    kg_send[...] = pack(key_grad[:128]).astype(BF16)
    kg1_send[...] = key_grad[248:]
    hand(kg_send, kg_recv, before)
    hand(kg1_send, kg1_recv, after)
    shifted_grad = pltpu.roll(key_grad, 1, 0)[128:]

    build_left(et, left)

    hops[3].wait_recv()
    hops[4].wait_recv()
    handed = pltpu.roll(unpack(kg_recv[...].astype(F32)), 1, 0)
    shifted_grad = shifted_grad + jnp.where(sub == 0, kg1_recv[7:8, :], handed)
    raw_grad = shifted_grad * cosine - pltpu.roll(shifted_grad, 32, 1) * sine
    raw_grad = jnp.where(keep, raw_grad, 0.0) * inverse
    right = jnp.concatenate(halves(raw_grad), 0).astype(BF16)

    def latent_part():
        for half in range(2):
            span = slice(half * 128, half * 128 + 128)
            part = jnp.dot(w_all[span, :], cot_all[...], preferred_element_type=F32)
            part = part + jnp.dot(sg_all[span, :], q_all[...], preferred_element_type=F32)
            if half == 0:
                lg_send[...] = part.astype(BF16)
                hand(lg_send, lg_recv, before)
            else:
                lg_own[...] = part

    def latent_out():
        hops[5].wait_recv()
        outlat_ref[...] = (lg_own[...] + lg_recv[...].astype(F32)).astype(BF16)

    def settle():
        for hop in hops:
            hop.wait_send()

    bufs = [bufs[8 * i : 8 * i + 8] for i in range(3)]
    reduce_scatter(
        at, right, outw_ref, scale, left, c_send, c_recv, own, c_ss, c_rs, ss, rs, bufs, latent_part, latent_out, settle
    )


def per_device(emb, doc_lengths, latent, q_latent, q_rope, cotangent, gain, w_rope):
    loss_scale = float(32 * 4096) ** (-0.5)
    vmem = pl.BlockSpec(memory_space=pltpu.VMEM)
    hbm = pl.BlockSpec(memory_space=pl.ANY)
    grad_latent, grad_rope_w = pl.pallas_call(
        lambda *refs: fused_kernel(loss_scale, *refs),
        out_shape=(
            pltpu.VMEM((128, 512), BF16),
            pltpu.VMEM((7, 64), F32),
        ),
        in_specs=[hbm] * 9,
        out_specs=(vmem, vmem),
        scratch_shapes=[
            pltpu.VMEM((1, 64), jnp.int32),
            pltpu.VMEM((128, 768), BF16),
            pltpu.VMEM((1, 7168), F32),
            pltpu.VMEM((128, 7168), BF16),
            pltpu.VMEM((64, 7168), BF16),
            pltpu.VMEM((256, 512), BF16),
            pltpu.VMEM((128, 4, 512), BF16),
            pltpu.VMEM((128, 256), BF16),
            pltpu.VMEM((128, 4, 512), BF16),
            pltpu.VMEM((512, 512), BF16),
            pltpu.VMEM((512, 512), BF16),
            pltpu.VMEM((64, 128), BF16),
            pltpu.VMEM((64, 128), BF16),
            pltpu.VMEM((8, 128), F32),
            pltpu.VMEM((8, 128), F32),
            pltpu.VMEM((64, 128), BF16),
            pltpu.VMEM((64, 128), BF16),
            pltpu.VMEM((8, 128), F32),
            pltpu.VMEM((8, 128), F32),
            pltpu.VMEM((128, 512), BF16),
            pltpu.VMEM((128, 512), BF16),
            pltpu.VMEM((128, 512), F32),
            pltpu.VMEM((256, 512), F32),
            pltpu.VMEM((256, 512), F32),
            pltpu.VMEM((256, 512), BF16),
            pltpu.VMEM((256, 512), BF16),
            pltpu.SemaphoreType.DMA((9,)),
            pltpu.SemaphoreType.DMA((6,)),
            pltpu.SemaphoreType.DMA((6,)),
        ]
        + rs_scratch(),
        compiler_params=pltpu.CompilerParams(
            collective_id=0, has_side_effects=True, vmem_limit_bytes=60 * 1024 * 1024
        ),
        name="fused",
    )(
        doc_lengths,
        jnp.asarray(rotary_tables()),
        gain[None],
        emb[0],
        w_rope.T,
        latent[0],
        q_latent[0],
        q_rope[0],
        cotangent[0],
    )
    return (grad_latent[None], grad_rope_w)


def solution(mesh):
    placed = (
        P("dp", "ctx", None),
        P("dp", None),
        P("dp", "ctx", None),
        P("dp", "ctx", None, None),
        P("dp", "ctx", None),
        P("dp", "ctx", None, None),
        P(),
        P(),
    )
    return jax.shard_map(
        per_device,
        mesh=mesh,
        in_specs=placed,
        out_specs=(P("dp", "ctx", None), P(("dp", "ctx"), None)),
        check_vma=False,
    )
```

```python
import numpy as np
import jax
import jax.numpy as jnp
from jax import lax
from jax.experimental import pallas as pl
from jax.experimental.pallas import tpu as pltpu
from jax.sharding import PartitionSpec as P

MESH = pl.DeviceIdType.MESH
F32 = jnp.float32
BF16 = jnp.bfloat16
UNITS = (2, 3, 2)
FIRST_UNIT = (0, 2, 5)
ROW_START = (0, 512, 1280)
SENDING = (1, 2, 0)
ORDER = (4, 3, 5, 2, 6, 1, 7)


def place():
    d, c = lax.axis_index("dp"), lax.axis_index("ctx")
    return {
        "core": c % 2,
        "x": (c // 2) % 8,
        "y": (d // 8) * 2 + c // 16,
        "z": d % 8,
    }


def device(at, **moved):
    p = {**at, **moved}
    return ((p["y"] // 2) * 8 + p["z"], ((p["y"] % 2) * 8 + p["x"]) * 2 + p["core"])


STAGES = (
    (("x", "z", "y"), ("y", "x", "z"), ("z", "x", "y")),
    (("x", "z", "y"), ("z", "x", "y"), ("y", "x", "z")),
)


def step_of(axis, i):
    if axis == "x":
        return i * 14
    if axis == "z":
        return i * 224
    return (i // 2) * 1792 + (i % 2) * 112


def build_left(et_ref, left_ref):
    def body(a, carry):
        for color, units in enumerate(UNITS):
            for unit in range(units):
                for q in range(2):
                    first, second, third = STAGES[q][color]
                    stride = step_of(second, 1)
                    for half in range(2):
                        for pair in range(2):
                            rows = []
                            for p in (2 * pair, 2 * pair + 1):
                                base = (
                                    step_of(first, a)
                                    + step_of(third, 2 * p + half)
                                    + q * 7
                                    + FIRST_UNIT[color]
                                    + unit
                                )
                                rows.append(et_ref[pl.ds(base, 8, stride=stride), :])
                            at = ROW_START[color] + a * (units * 32) + unit * 32 + pair * 16
                            left_ref[
                                q, pl.ds(pl.multiple_of(at, 16), 16), half * 128 : half * 128 + 128
                            ] = jnp.concatenate(rows, 0).astype(BF16)
        return carry

    lax.fori_loop(0, 8, body, 0)


def rs_scratch():
    shapes = [
        pltpu.VMEM((7168, 128), F32),
        pltpu.VMEM((2, 1792, 256), BF16),
        pltpu.VMEM((1792, 128), BF16),
        pltpu.VMEM((1792, 128), BF16),
        pltpu.VMEM((1792, 128), F32),
        pltpu.SemaphoreType.DMA((3,)),
        pltpu.SemaphoreType.DMA((3,)),
        pltpu.SemaphoreType.DMA((3, 3, 8)),
        pltpu.SemaphoreType.DMA((3, 3, 8)),
    ]
    for n in UNITS:
        shapes += [
            pltpu.VMEM((8, n * 32, 128), BF16),
            pltpu.VMEM((8, n * 32, 128), BF16),
            pltpu.VMEM((n * 32, 128), F32),
            pltpu.VMEM((8, n * 4, 128), BF16),
            pltpu.VMEM((8, n * 4, 128), BF16),
            pltpu.VMEM((n * 4, 128), F32),
            pltpu.VMEM((4, n, 128), F32),
            pltpu.VMEM((8, n, 128), F32),
        ]
    return shapes


def greet(at, barrier):
    for step in ORDER:
        for axis in ("x", "y", "z"):
            pl.semaphore_signal(
                barrier,
                inc=1,
                device_id=device(at, **{axis: (at[axis] + step) % 8}),
                device_id_type=MESH,
            )
    pl.semaphore_signal(barrier, inc=1, device_id=device(at, core=1 - at["core"]), device_id_type=MESH)


GREETED = 22


def reduce_scatter(
    at, right, out_ref, scale, left_ref, c_send, c_recv, own, c_ss, c_rs, ss, rs, bufs, under_first, under_second, under_third
):
    core = at["core"]
    partner = device(at, core=1 - core)
    pending = []
    core_copies = {}
    for color in SENDING:
        n = UNITS[color]
        rows = pl.ds(ROW_START[color], n * 256)
        c_send[rows, :] = jnp.dot(
            left_ref[1 - core, rows, :], right, preferred_element_type=F32
        ).astype(BF16)
        copy = pltpu.make_async_remote_copy(
            src_ref=c_send.at[rows],
            dst_ref=c_recv.at[rows],
            send_sem=c_ss.at[color],
            recv_sem=c_rs.at[color],
            device_id=partner,
            device_id_type=MESH,
        )
        copy.start()
        core_copies[color] = copy

    def by_core(low, high):
        return low + core * (high - low)

    def spot(color, stage):
        return by_core(*(at[STAGES[q][color][stage]] for q in range(2)))

    def peer(color, stage, to):
        low, high = (device(at, **{STAGES[q][color][stage]: to}) for q in range(2))
        return tuple(by_core(a, b) for a, b in zip(low, high))

    def send(color, stage, source_of, target):
        for step in ORDER:
            to = (spot(color, stage) + step) % 8
            copy = pltpu.make_async_remote_copy(
                src_ref=source_of(to),
                dst_ref=target.at[step],
                send_sem=ss.at[color, stage, step],
                recv_sem=rs.at[color, stage, step],
                device_id=peer(color, stage, to),
                device_id_type=MESH,
            )
            copy.start()
            pending.append((color, stage, copy))

    def arrived(color, stage):
        for c, s, copy in pending:
            if (c, s) == (color, stage):
                copy.wait_recv()

    def total(first, target):
        value = first.astype(F32)
        for step in range(1, 8):
            value = value + target[step].astype(F32)
        return value

    for color in SENDING:
        n = UNITS[color]
        s1, r1, t1, s2, r2, t2, s3, r3 = bufs[color]
        span = pl.ds(ROW_START[color], n * 256)
        own[span, :] = jnp.dot(left_ref[core, span, :], right, preferred_element_type=F32)
        core_copies[color].wait_recv()
        for a in range(8):
            rows = pl.ds(ROW_START[color] + a * n * 32, n * 32)
            s1[a] = (own[rows, :] + c_recv[rows, :].astype(F32)).astype(BF16)
        send(color, 0, lambda to: s1.at[to], r1)
    under_first()
    for color, n in enumerate(UNITS):
        s1, r1, t1, s2, r2, t2, s3, r3 = bufs[color]
        arrived(color, 0)
        t1[...] = total(s1[spot(color, 0)], r1)
        for b in range(8):
            s2[b] = t1[pl.ds(b, n * 4, stride=8), :].astype(BF16)
        send(color, 1, lambda to: s2.at[to], r2)
    under_second()
    for color, n in enumerate(UNITS):
        s1, r1, t1, s2, r2, t2, s3, r3 = bufs[color]
        arrived(color, 1)
        t2[...] = total(s2[spot(color, 1)], r2)
        for p in range(4):
            s3[p] = t2[pl.ds(p, n, stride=4), :]
        send(color, 2, lambda to: s3.at[to // 2], r3)
    for copy in core_copies.values():
        copy.wait_send()
    for color, stage, copy in pending:
        if stage < 2:
            copy.wait_send()
    under_third()
    for color, n in enumerate(UNITS):
        s1, r1, t1, s2, r2, t2, s3, r3 = bufs[color]
        arrived(color, 2)
        last = spot(color, 2)
        value = total(s3[last // 2], r3) * scale
        value = jnp.where(last % 2 == 0, value, pltpu.roll(value, 64, 1))
        out_ref[FIRST_UNIT[color] : FIRST_UNIT[color] + n, :] = value[:, :64]
    for color, stage, copy in pending:
        if stage == 2:
            copy.wait_send()


score_scale = 192.0 ** (-0.5)
norm_eps = 1e-06
MERGED = 2


def rotary_tables():
    frequency = (10000.0 ** (-np.arange(32, dtype=np.float32) / 32)).astype(np.float32)
    angles = np.arange(128, dtype=np.float32)[:, None] * frequency[None, :]
    cosine = np.cos(angles.astype(np.float64)).astype(np.float32)
    sine = np.sin(angles.astype(np.float64)).astype(np.float32)
    rest = np.concatenate([np.tile(cosine, 4), -sine, sine, -sine, sine], 1)
    parts = []
    for _ in range(3):
        part = rest.astype(jnp.bfloat16)
        parts.append(part)
        rest = rest - part.astype(np.float32)
    return np.concatenate(parts, 1)


def cols(left, right):
    return lax.dot_general(left, right, (((1,), (1,)), ((), ())), preferred_element_type=F32)


def halves(value):
    low = lax.broadcasted_iota(jnp.int32, value.shape, 1) < 64
    return jnp.where(low, value, 0.0), jnp.where(low, 0.0, value)


def pack(value):
    low = lax.broadcasted_iota(jnp.int32, (64, 128), 1) < 64
    return jnp.where(low, value[:64], value[64:128])


def unpack(value):
    low = lax.broadcasted_iota(jnp.int32, (64, 128), 1) < 64
    other = pltpu.roll(value, 64, 1)
    return jnp.concatenate([jnp.where(low, value, other), jnp.where(low, other, value)], 0)


def fused_kernel(
    scale,
    lengths_hbm,
    table_hbm,
    gain_hbm,
    emb_hbm,
    w_hbm,
    lat_hbm,
    q_hbm,
    qr_hbm,
    cot_hbm,
    outlat_ref,
    outw_ref,
    lengths_ref,
    table_ref,
    gain_ref,
    emb,
    w_t,
    keys,
    q_in,
    qr,
    cot_in,
    q_all,
    cot_all,
    kr_send,
    kr_recv,
    kr1_send,
    kr1_recv,
    kg_send,
    kg_recv,
    kg1_send,
    kg1_recv,
    lg_send,
    lg_recv,
    lg_own,
    s_all,
    d_all,
    w_all,
    sg_all,
    local_sem,
    ns,
    nr,
    et,
    left,
    c_send,
    c_recv,
    own,
    c_ss,
    c_rs,
    ss,
    rs,
    *bufs,
):
    at = place()
    dp, ctx = lax.axis_index("dp"), lax.axis_index("ctx")
    after, before = (dp, (ctx + 1) % 32), (dp, (ctx + 31) % 32)
    loads = []
    pairs = (
        (lengths_hbm, lengths_ref),
        (gain_hbm, gain_ref),
        (emb_hbm, emb),
        (w_hbm, w_t),
        (table_hbm, table_ref),
        (lat_hbm, keys.at[128:256]),
        (q_hbm, q_in),
        (cot_hbm, cot_in),
        (qr_hbm, qr),
    )
    for i, (source, target) in enumerate(pairs):
        copy = pltpu.make_async_copy(source, target, local_sem.at[i])
        copy.start()
        loads.append(copy)
    barrier = pltpu.get_barrier_semaphore()
    greet(at, barrier)
    for near in (after, before):
        pl.semaphore_signal(barrier, inc=1, device_id=near, device_id_type=MESH)

    hops = []

    def hand(source, target, to):
        i = len(hops)
        copy = pltpu.make_async_remote_copy(
            src_ref=source,
            dst_ref=target,
            send_sem=ns.at[i],
            recv_sem=nr.at[i],
            device_id=to,
            device_id_type=MESH,
        )
        copy.start()
        hops.append(copy)

    offset = ctx * 128
    loads[0].wait()
    lengths = lengths_ref[...].astype(F32)
    sub64 = lax.broadcasted_iota(jnp.int32, (64, 64), 0)
    lane64 = lax.broadcasted_iota(jnp.int32, (64, 64), 1)
    ends = jnp.sum(jnp.where(lane64 <= sub64, lengths, 0.0), 1, keepdims=True)
    place_row = (offset + lax.broadcasted_iota(jnp.int32, (1, 128), 1)).astype(F32)
    start_row = jnp.max(jnp.where(ends <= place_row, ends, 0.0), 0, keepdims=True)
    shift_start = jnp.max(jnp.where(ends <= place_row - 1.0, ends, 0.0), 0, keepdims=True)
    ended = jnp.max(jnp.where(ends == place_row, 1.0, 0.0), 0, keepdims=True)
    keep_row = jnp.where((place_row >= 1.0) & (place_row < 4096.0), 1.0 - ended, 0.0)
    sub = lax.broadcasted_iota(jnp.int32, (128, 128), 0)
    lane = lax.broadcasted_iota(jnp.int32, (128, 128), 1)
    eye = sub == lane
    start_col = jnp.sum(jnp.where(eye, shift_start, 0.0), 1, keepdims=True)
    keep = jnp.sum(jnp.where(eye, keep_row, 0.0), 1, keepdims=True) > 0.5
    pos_lane = (offset - 1 + sub).astype(F32) - start_col
    chosen = jnp.where(pos_lane == lane.astype(F32), 1.0, 0.0).astype(BF16)

    loads[1].wait()
    loads[2].wait()
    loads[3].wait()

    def spans(i):
        for k in range(8):
            yield pl.ds(pl.multiple_of(i * 1024 + k * 128, 128), 128)

    def prepare(turned):
        def body(i, squares):
            for span in spans(i):
                scale_here = gain_ref[:, span]
                w_t[:, span] = (w_t[:, span].astype(F32) * scale_here).astype(BF16)
                value = emb[:, span].astype(F32)
                squares = squares + value * value
                if turned:
                    et[span, :] = (value * scale_here).T
            return squares

        return body

    def turn(i, carry):
        for span in spans(i):
            et[span, :] = (emb[:, span].astype(F32) * gain_ref[:, span]).T
        return carry

    squares = lax.fori_loop(0, MERGED, prepare(True), jnp.zeros((128, 128), F32))
    squares = lax.fori_loop(MERGED, 7, prepare(False), squares)
    pl.semaphore_wait(barrier, GREETED + 2)
    hand(lat_hbm, keys.at[0:128], after)
    raw = cols(emb[...], w_t[...])
    inverse = lax.rsqrt(jnp.sum(squares, 1, keepdims=True) / 7168.0 + norm_eps)
    loads[4].wait()
    table = jnp.dot(chosen, table_ref[...], preferred_element_type=F32)
    table = table[:, :256] + table[:, 256:512] + table[:, 512:]
    cosine, sine = table[:, :128], table[:, 128:]
    raw = raw * inverse
    raw = jnp.where(keep, jnp.concatenate([raw, raw], 1), 0.0)
    key_rope = (raw * cosine + pltpu.roll(raw, 32, 1) * sine).astype(BF16).astype(F32)
    kr_send[...] = pack(key_rope).astype(BF16)
    kr1_send[...] = key_rope[0:8]
    hand(kr_send, kr_recv, after)
    hand(kr1_send, kr1_recv, before)

    for i in (5, 6, 7, 8):
        loads[i].wait()
    q_all[...] = pltpu.einshape("thd->htd", q_in[...]).reshape(512, 512)
    cot_all[...] = pltpu.einshape("thd->htd", cot_in[...]).reshape(512, 512)
    lax.fori_loop(MERGED, 7, turn, 0)

    hops[0].wait_recv()
    s_all[...] = cols(keys[...], q_all[...])
    d_all[...] = cols(keys[...], cot_all[...])
    hops[1].wait_recv()
    hops[2].wait_recv()
    all_rope = jnp.concatenate([unpack(kr_recv[...].astype(F32)), key_rope], 0)
    final = lax.broadcasted_iota(jnp.int32, (256, 128), 0) == 255
    all_rope = jnp.where(final, kr1_recv[0:1, :], pltpu.roll(all_rope, 255, 0))
    ropes = [h.astype(BF16) for h in halves(all_rope)]
    key_place = (offset - 128 + lax.broadcasted_iota(jnp.int32, (256, 128), 0)).astype(F32)
    allowed = (key_place >= start_row) & (key_place <= place_row)
    parts = [jnp.zeros((256, 128), F32)] * 2
    for h in range(4):
        span = slice(h * 128, h * 128 + 128)
        query_rope = qr[:, (h // 2) * 128 : (h // 2) * 128 + 128]
        score = (s_all[:, span] + cols(ropes[h % 2], query_rope)) * score_scale
        score = jnp.where(allowed, score, -1e30)
        highest = jnp.max(score, 0, keepdims=True)
        exponent = jnp.where(allowed, jnp.exp(score - highest), 0.0)
        probs = exponent / jnp.sum(exponent, 0, keepdims=True)
        w_all[:, span] = probs.astype(BF16)
        dprobs = d_all[:, span]
        centre = jnp.sum(probs * dprobs, 0, keepdims=True)
        score_grad = (score_scale * probs * (dprobs - centre)).astype(BF16)
        sg_all[:, span] = score_grad
        parts[h % 2] = parts[h % 2] + jnp.dot(score_grad, query_rope, preferred_element_type=F32)
    wide = lax.broadcasted_iota(jnp.int32, (256, 128), 1)
    key_grad = jnp.where(wide < 64, parts[0], parts[1])
    key_grad = key_grad + pltpu.roll(key_grad, 64, 1)
    kg_send[...] = pack(key_grad[:128]).astype(BF16)
    kg1_send[...] = key_grad[248:]
    hand(kg_send, kg_recv, before)
    hand(kg1_send, kg1_recv, after)
    shifted_grad = pltpu.roll(key_grad, 1, 0)[128:]

    build_left(et, left)

    hops[3].wait_recv()
    hops[4].wait_recv()
    handed = pltpu.roll(unpack(kg_recv[...].astype(F32)), 1, 0)
    shifted_grad = shifted_grad + jnp.where(sub == 0, kg1_recv[7:8, :], handed)
    raw_grad = shifted_grad * cosine - pltpu.roll(shifted_grad, 32, 1) * sine
    raw_grad = jnp.where(keep, raw_grad, 0.0) * inverse
    right = jnp.concatenate(halves(raw_grad), 0).astype(BF16)

    def latent_part():
        for half in range(2):
            span = slice(half * 128, half * 128 + 128)
            part = jnp.dot(w_all[span, :], cot_all[...], preferred_element_type=F32)
            part = part + jnp.dot(sg_all[span, :], q_all[...], preferred_element_type=F32)
            if half == 0:
                lg_send[...] = part.astype(BF16)
                hand(lg_send, lg_recv, before)
            else:
                lg_own[...] = part

    def latent_out():
        hops[5].wait_recv()
        outlat_ref[...] = (lg_own[...] + lg_recv[...].astype(F32)).astype(BF16)

    def settle():
        latent_out()
        for hop in hops:
            hop.wait_send()

    bufs = [bufs[8 * i : 8 * i + 8] for i in range(3)]
    reduce_scatter(
        at, right, outw_ref, scale, left, c_send, c_recv, own, c_ss, c_rs, ss, rs, bufs, lambda: None, latent_part, settle
    )


def per_device(emb, doc_lengths, latent, q_latent, q_rope, cotangent, gain, w_rope):
    loss_scale = float(32 * 4096) ** (-0.5)
    vmem = pl.BlockSpec(memory_space=pltpu.VMEM)
    hbm = pl.BlockSpec(memory_space=pl.ANY)
    grad_latent, grad_rope_w = pl.pallas_call(
        lambda *refs: fused_kernel(loss_scale, *refs),
        out_shape=(
            pltpu.VMEM((128, 512), BF16),
            pltpu.VMEM((7, 64), F32),
        ),
        in_specs=[hbm] * 9,
        out_specs=(vmem, vmem),
        scratch_shapes=[
            pltpu.VMEM((1, 64), jnp.int32),
            pltpu.VMEM((128, 768), BF16),
            pltpu.VMEM((1, 7168), F32),
            pltpu.VMEM((128, 7168), BF16),
            pltpu.VMEM((64, 7168), BF16),
            pltpu.VMEM((256, 512), BF16),
            pltpu.VMEM((128, 4, 512), BF16),
            pltpu.VMEM((128, 256), BF16),
            pltpu.VMEM((128, 4, 512), BF16),
            pltpu.VMEM((512, 512), BF16),
            pltpu.VMEM((512, 512), BF16),
            pltpu.VMEM((64, 128), BF16),
            pltpu.VMEM((64, 128), BF16),
            pltpu.VMEM((8, 128), F32),
            pltpu.VMEM((8, 128), F32),
            pltpu.VMEM((64, 128), BF16),
            pltpu.VMEM((64, 128), BF16),
            pltpu.VMEM((8, 128), F32),
            pltpu.VMEM((8, 128), F32),
            pltpu.VMEM((128, 512), BF16),
            pltpu.VMEM((128, 512), BF16),
            pltpu.VMEM((128, 512), F32),
            pltpu.VMEM((256, 512), F32),
            pltpu.VMEM((256, 512), F32),
            pltpu.VMEM((256, 512), BF16),
            pltpu.VMEM((256, 512), BF16),
            pltpu.SemaphoreType.DMA((9,)),
            pltpu.SemaphoreType.DMA((6,)),
            pltpu.SemaphoreType.DMA((6,)),
        ]
        + rs_scratch(),
        compiler_params=pltpu.CompilerParams(
            collective_id=0, has_side_effects=True, vmem_limit_bytes=60 * 1024 * 1024
        ),
        name="fused",
    )(
        doc_lengths,
        jnp.asarray(rotary_tables()),
        gain[None],
        emb[0],
        w_rope.T,
        latent[0],
        q_latent[0],
        q_rope[0],
        cotangent[0],
    )
    return (grad_latent[None], grad_rope_w)


def solution(mesh):
    placed = (
        P("dp", "ctx", None),
        P("dp", None),
        P("dp", "ctx", None),
        P("dp", "ctx", None, None),
        P("dp", "ctx", None),
        P("dp", "ctx", None, None),
        P(),
        P(),
    )
    return jax.shard_map(
        per_device,
        mesh=mesh,
        in_specs=placed,
        out_specs=(P("dp", "ctx", None), P(("dp", "ctx"), None)),
        check_vma=False,
    )
```
